32 devices in a mesh: parts: 2 (over y), lon: 4 (over z), lat: 2 (over core), chan: 2 (over x).
Axes of the slice: x: 2, y: 2, z: 4, core: 2. Of those that a mesh axis runs over, the one named last changes fastest.
Arguments:
- fine_act: bfloat16 [384, 896, 256], P(('parts', 'lat', 'chan'), 'lon'), parts along dimension 0, may hold values from -6 to 6
- coarse_grad: bfloat16 [192, 448, 128], P(('parts', 'lat'), 'lon', 'chan'), parts along dimension 0, may hold values from -6 to 6
- kernel: bfloat16 [3, 3, 256, 128], replicated, may hold values from -0.125 to 0.125
Outputs:
- input_grad: bfloat16 [384, 896, 256], P(('parts', 'lat', 'chan'), 'lon'), parts along dimension 0
- kernel_grad: float32 [6, 3, 256, 128], P('parts'), parts along dimension 0
The draws below stay inside these ranges and needn't reach their ends.
There are 2 independent parts, one for each index of `parts`. The reference program is written for one: setup_inputs(seed, part) draws one part's arguments, and reference() takes and returns one part's arrays. A program takes and returns all parts, laid end to end along the dimension named above; an argument that names none is the same for every part. Nothing has to cross between parts.
All inputs are finite; a program needn't handle non-finite values.
Results may differ from the reference program's by a relative error of at most 0.001.
Values may be sent and summed in bfloat16 or wider, within the bound.
A program may use at most 64 MiB of HBM per device.

```python
import math
import jax
import jax.numpy as jnp

CIN = 256
COUT = 128
NLAT = 192
NLON = 896
CLAT = 96
CLON = 448


def levels(rng, extent, cuts, smallest, largest):
    loudness = 1.0
    for position, blocks in cuts:
        draws = jax.random.uniform(jax.random.fold_in(jax.random.fold_in(rng, 6), position), (blocks,), jnp.float32, smallest / len(cuts), largest / len(cuts))
        loudness = loudness * jnp.repeat(jnp.exp(draws), extent[position] // blocks).reshape((-1,) + (1,) * (len(extent) - 1 - position))
    return loudness


def scatter_about(rng, extent, width, bound, split=(), dtype=jnp.bfloat16):
    factor_of = levels(rng, extent, split, -0.22, 0.18) if split else 1.0
    values = jax.random.normal(rng, extent, jnp.float32) * width * factor_of
    return jnp.minimum(jnp.maximum(values, -bound), bound).astype(dtype)


def setup_inputs(seed: int = 0, part: int = 0) -> dict:
    key_list = jax.random.split(jax.random.key(seed), 4)
    part_keys = jax.random.split(jax.random.fold_in(key_list[3], part), 4)
    return {
        "fine_act": scatter_about(part_keys[0], (NLAT, NLON, CIN), 1.0, 6.0, ((0, 4), (1, 4))),
        "coarse_grad": scatter_about(part_keys[1], (CLAT, CLON, COUT), 1.0, 6.0, ((0, 2), (1, 4), (2, 2))),
        "kernel": scatter_about(key_list[2], (3, 3, CIN, COUT), (9 * CIN) ** -0.5, 0.125),
    }


def reference(fine_act, coarse_grad, kernel):
    even_act = fine_act[::2, ::2, :]
    even_flat = even_act.reshape(CLAT * CLON, CIN)
    padded = jnp.pad(coarse_grad, ((1, 1), (0, 0), (0, 0)))
    padded = jnp.concatenate([padded[:, -1:], padded, padded[:, :1]], axis=1)
    total = jnp.zeros((CLAT * CLON, CIN), jnp.float32)
    partial_list = []
    for tap_row in range(3):
        for tap_col in range(3):
            shifted = padded[2 - tap_row:2 - tap_row + CLAT, 2 - tap_col:2 - tap_col + CLON].reshape(CLAT * CLON, COUT)
            total = total + jnp.dot(shifted, kernel[tap_row, tap_col].T, preferred_element_type=jnp.float32)
            partial_list.append(jnp.dot(even_flat.T, shifted, preferred_element_type=jnp.float32))
    even_grad = total.astype(jnp.bfloat16).reshape(CLAT, CLON, CIN)
    input_grad = jnp.zeros((NLAT, NLON, CIN), jnp.bfloat16).at[::2, ::2, :].set(even_grad)
    kernel_grad = jnp.stack(partial_list).reshape(3, 3, CIN, COUT) * (1.0 / math.sqrt(CLAT * CLON))
    return (input_grad, kernel_grad)
```

```python
import functools
import math

import jax
import jax.numpy as jnp
from jax import lax
from jax.experimental import pallas as pl
from jax.experimental.pallas import tpu as pltpu
from jax.sharding import PartitionSpec as P

MESH = pl.DeviceIdType.MESH
LANES = 128
F32 = jnp.float32
BF16 = jnp.bfloat16
TAP_ORDER = (1, 0, 2)
AXES = ("lon", "lat", "chan")


def one_hot(shape, test):
    rows = lax.broadcasted_iota(jnp.int32, shape, 0)
    cols = lax.broadcasted_iota(jnp.int32, shape, 1)
    return jnp.where(test(rows, cols), 1.0, 0.0).astype(BF16)


def share(rows, peers, unit):
    for size in range(unit, rows + 1, unit):
        if rows % size == 0 and rows // size <= peers:
            return size
    raise ValueError("no share")


def stage_plan(rows, order, sizes):
    plan = []
    for position, axis in enumerate(order):
        unit = 8
        for later in order[position + 1:]:
            unit *= sizes[later] if later != "lon" else 1
        part = share(rows, sizes[axis], unit)
        plan.append((axis, part, rows // part))
        rows = part
    return plan


def grads_kernel(
    sizes, half_rows, half_cols, out_ch, scale,
    fine, cg, kernel, rows_out, kg_out,
    fbuf, kcat, tiles, taps, even_t, edge_out, edge_in, spots, acc, row_sem, *rest,
):
    landing, (local_sem, tile_recv, tile_send, edge_send, edge_recv, red_send, red_recv, gat_send, gat_recv) = rest[:-9], rest[-9:]
    lon_n, lat_n, chan_n = (sizes[a] for a in AXES)
    me = {a: lax.axis_index(a) for a in AXES}
    lat, chan = me["lat"], me["chan"]
    h = half_rows
    group = group_size(h + 2)
    spans = [(max(1, q * group), min(h + 1, (q + 1) * group)) for q in range((h + 2) // group)]
    width = cg.shape[1]
    in_ch = fbuf.shape[2]
    mine = pl.ds(pl.multiple_of(chan * width, width), width)

    def other(axis, step):
        return lax.rem(me[axis] + step, sizes[axis])

    local = [pltpu.make_async_copy(fine.at[:, 0], fbuf, local_sem.at[0])]
    for r in range(3):
        for s in range(3):
            local.append(
                pltpu.make_async_copy(
                    kernel.at[r, s], kcat.at[r, :, pl.ds(s * out_ch, out_ch)], local_sem.at[1 + 3 * r + s]
                )
            )
    for copy in local:
        copy.start()

    is_top = jnp.logical_and(lat == 0, chan == 0)
    is_bottom = jnp.logical_and(lat == lat_n - 1, chan == chan_n - 1)
    for q, (lo, hi) in enumerate(spans):
        pltpu.make_async_copy(
            cg.at[pl.ds(chan * h + lo - 1, hi - lo)], tiles.at[pl.ds(lo, hi - lo), mine], tile_recv.at[2 + q]
        ).start()

    @pl.when(chan > 0)
    def _():
        pltpu.make_async_copy(cg.at[chan * h - 1], tiles.at[0, mine], tile_recv.at[0]).start()

    @pl.when(chan < chan_n - 1)
    def _():
        pltpu.make_async_copy(cg.at[(chan + 1) * h], tiles.at[h + 1, mine], tile_recv.at[1]).start()

    barrier = pltpu.get_barrier_semaphore()
    greeted = 0
    for dl in range(lat_n):
        for dc in range(chan_n):
            if dl or dc:
                pl.semaphore_signal(
                    barrier, inc=1, device_id={"lat": other("lat", dl), "chan": other("chan", dc)}, device_id_type=MESH
                )
                greeted += 1
    for d in range(1, lon_n):
        pl.semaphore_signal(barrier, inc=1, device_id={"lon": other("lon", d)}, device_id_type=MESH)
        greeted += 1
    pl.semaphore_wait(barrier, greeted)

    sends = []

    def send(condition, src, dst, send_sem, recv_sem, where):
        copy = pltpu.make_async_remote_copy(
            src_ref=src, dst_ref=dst, send_sem=send_sem, recv_sem=recv_sem, device_id=where, device_id_type=MESH
        )
        if condition is None:
            copy.start()
        else:
            pl.when(condition)(lambda: copy.start())
        sends.append((condition, copy))

    slot = 0
    for d in range(1, chan_n):
        p = other("chan", d)
        send(p > 0, cg.at[jnp.maximum(p * h - 1, 0)], tiles.at[0, mine], tile_send.at[slot], tile_recv.at[0], {"chan": p})
        slot += 1
    send(
        lat < lat_n - 1, cg.at[chan_n * h - 1], tiles.at[0, mine], tile_send.at[slot], tile_recv.at[0],
        {"lat": jnp.minimum(lat + 1, lat_n - 1), "chan": 0},
    )
    send(
        lat > 0, cg.at[0], tiles.at[h + 1, mine], tile_send.at[slot + 1], tile_recv.at[1],
        {"lat": jnp.maximum(lat - 1, 0), "chan": chan_n - 1},
    )
    slot += 2
    for q, (lo, hi) in enumerate(spans):
        for d in range(1, chan_n):
            p = other("chan", d)
            send(
                None, cg.at[pl.ds(p * h + lo - 1, hi - lo)], tiles.at[pl.ds(lo, hi - lo), mine],
                tile_send.at[slot], tile_recv.at[2 + q], {"chan": p},
            )
            slot += 1
    for d in range(1, chan_n):
        p = other("chan", d)
        send(
            p < chan_n - 1, cg.at[jnp.minimum((p + 1) * h, chan_n * h - 1)], tiles.at[h + 1, mine],
            tile_send.at[slot], tile_recv.at[1], {"chan": p},
        )
        slot += 1

    local[0].wait()
    pick = one_hot((2 * half_cols, LANES), lambda row, col: row == 2 * col)

    def take_even(i, _):
        picked = lax.dot_general(fbuf[i], pick, (((0,), (0,)), ((), ())), preferred_element_type=F32)
        even_t[:, pl.ds(pl.multiple_of(i * LANES, LANES), LANES)] = picked.astype(BF16)
        return 0

    lax.fori_loop(0, h, take_even, 0)

    @pl.when(is_top)
    def _():
        tiles[0] = jnp.zeros(tiles.shape[1:], BF16)

    @pl.when(is_bottom)
    def _():
        tiles[h + 1] = jnp.zeros(tiles.shape[1:], BF16)

    def make_spots(k, _):
        at = pl.ds(pl.multiple_of(k * LANES, LANES), LANES)
        for side, lane in ((0, half_cols - 1), (1, 0)):
            spots[side, :, at] = one_hot((LANES, LANES), lambda row, col: jnp.logical_and(row == k, col == lane))
        return 0

    lax.fori_loop(0, h + 2, make_spots, 0)

    def shifted_source(row, col):
        s, j = col // LANES, col % LANES
        return jnp.logical_and(row == j + 1 - s, j < half_cols)

    shift = one_hot((half_cols, 3 * LANES), shifted_source)

    for q, (lo, hi) in enumerate(spans):
        if q == 0:

            @pl.when(jnp.logical_not(is_top))
            def _():
                pltpu.make_async_copy(tiles.at[0], tiles.at[0], tile_recv.at[0]).wait()

        pltpu.make_async_copy(tiles.at[pl.ds(lo, hi - lo)], tiles.at[pl.ds(lo, hi - lo)], tile_recv.at[2 + q]).wait()
        if q == len(spans) - 1:

            @pl.when(jnp.logical_not(is_bottom))
            def _():
                pltpu.make_async_copy(tiles.at[h + 1], tiles.at[h + 1], tile_recv.at[1]).wait()

        block = tiles[pl.ds(q * group, group)].reshape(group * out_ch, half_cols)
        moved = jnp.dot(block, shift, preferred_element_type=F32).astype(BF16)
        for k in range(group):
            for s in range(3):
                taps[pl.ds(s * out_ch, out_ch), pl.ds((q * group + k) * LANES, LANES)] = moved[
                    k * out_ch:(k + 1) * out_ch, s * LANES:(s + 1) * LANES
                ]

    centre = taps[pl.ds(out_ch, out_ch), :]
    for side in range(2):
        edge_out[side] = lax.dot_general(
            centre, spots[side], (((1,), (1,)), ((), ())), preferred_element_type=F32
        ).astype(BF16)
    send(None, edge_out.at[0], edge_in.at[0], edge_send.at[0], edge_recv.at[0], {"lon": other("lon", 1)})
    send(None, edge_out.at[1], edge_in.at[1], edge_send.at[1], edge_recv.at[1], {"lon": other("lon", lon_n - 1)})

    def inject(s, came, spot):
        pltpu.make_async_copy(edge_in.at[came], edge_in.at[came], edge_recv.at[came]).wait()
        at = pl.ds(s * out_ch, out_ch)
        put = jnp.dot(edge_in[came], spots[spot], preferred_element_type=F32)
        taps[at, :] = (taps[at, :].astype(F32) + put).astype(BF16)

    counter = {"red": 0, "gat": 0, "land": 0}
    blocks = reduce_blocks(acc.shape[0], sizes)
    state = []

    def weight_terms(block):
        s = TAP_ORDER[block]
        for r in range(3):
            acc[pl.ds((3 * block + r) * in_ch, in_ch), :] = lax.dot_general(
                even_t[...], taps[pl.ds(s * out_ch, out_ch), pl.ds((2 - r) * LANES, h * LANES)],
                (((1,), (1,)), ((), ())), preferred_element_type=F32,
            )

    def owner_of(index, axis, owners):
        if owners == sizes[axis]:
            return None, index
        return index < owners, jnp.minimum(index, owners - 1)

    def scatter(block, stage):
        start, plan = blocks[block]
        axis, part, owners = plan[stage]
        base = start if stage == 0 else state[block]["base"]
        if stage == 0:
            state.append({"stack": []})
        land = landing[counter["land"]]
        counter["land"] += 1
        arrivals = []
        for d in range(1, sizes[axis]):
            p = other(axis, d)
            n = counter["red"]
            counter["red"] += 1
            toowner, target = owner_of(p, axis, owners)
            send(
                toowner, acc.at[pl.ds(pl.multiple_of(base + target * part, 8), part)], land.at[d - 1],
                red_send.at[n], red_recv.at[n], {axis: p},
            )
            arrivals.append(n)
        amowner, own = owner_of(me[axis], axis, owners)
        state[block]["base"] = base + own * part
        state[block]["stack"].append((axis, part, owners, base, amowner, own))
        state[block]["open"] = (land, arrivals, amowner, part)

    def add_up(block, final=False):
        land, arrivals, amowner, part = state[block]["open"]
        at = pl.ds(pl.multiple_of(state[block]["base"], 8), part)

        def absorb():
            for position, n in enumerate(arrivals):
                pltpu.make_async_copy(land.at[position], land.at[position], red_recv.at[n]).wait()
            total = acc[at, :]
            for position in range(len(arrivals)):
                total = total + land[position]
            if final:
                kg_out[at, :] = total * scale
            else:
                acc[at, :] = total

        if amowner is None:
            absorb()
        else:
            pl.when(amowner)(absorb)

    def gather(block, stage):
        axis, part, owners, base, amowner, own = state[block]["stack"][stage]
        at = pl.ds(pl.multiple_of(base + own * part, 8), part)
        waits = []
        for d in range(1, sizes[axis]):
            n = counter["gat"]
            counter["gat"] += 1
            send(amowner, kg_out.at[at], kg_out.at[at], gat_send.at[n], gat_recv.at[n], {axis: other(axis, d)})
            fromowner, source = owner_of(other(axis, sizes[axis] - d), axis, owners)
            there = kg_out.at[pl.ds(pl.multiple_of(base + source * part, 8), part)]
            waits.append((fromowner, pltpu.make_async_copy(there, there, gat_recv.at[n])))
        state[block]["waits"] = waits

    def gathered(block):
        for condition, copy in state[block]["waits"]:
            if condition is None:
                copy.wait()
            else:
                pl.when(condition)(lambda copy=copy: copy.wait())

    spread = one_hot((2 * half_cols, LANES), lambda row, col: row == 2 * col)

    def make_even_grad(i, _):
        total = jnp.zeros((in_ch, 2 * LANES), F32)
        for r in range(3):
            at = pl.ds(pl.multiple_of(i * 2 * LANES + (2 - r) * LANES, LANES), 2 * LANES)
            total = total + jnp.dot(kcat[r], taps[:, at], preferred_element_type=F32)
        total = total.astype(BF16)
        for k in range(2):
            row = lax.dot_general(
                spread, total[:, k * LANES:(k + 1) * LANES], (((1,), (1,)), ((), ())), preferred_element_type=F32
            )
            rows_out[2 * i + k] = row.astype(BF16)
        return 0

    pairs = h // 2
    row_copies = []
    cuts = [pairs * k // 4 for k in range(5)]

    def even_grads(k):
        lax.fori_loop(cuts[k], cuts[k + 1], make_even_grad, 0)

    weight_terms(0)
    scatter(0, 0)
    inject(0, 1, 0)
    add_up(0)
    scatter(0, 1)
    weight_terms(1)
    scatter(1, 0)
    inject(2, 0, 1)
    add_up(1)
    scatter(1, 1)
    add_up(0)
    scatter(0, 2)
    weight_terms(2)
    scatter(2, 0)
    for copy in local[1:]:
        copy.wait()
    add_up(2)
    scatter(2, 1)
    add_up(1)
    scatter(1, 2)
    even_grads(0)
    add_up(2)
    scatter(2, 2)
    for block in range(3):
        even_grads(block + 1)
        add_up(block, True)
        gather(block, 2)
    for stage in (1, 0):
        for block in range(3):
            gathered(block)
            gather(block, stage)
    for block in range(3):
        gathered(block)

    for copy in row_copies:
        copy.wait()
    for condition, copy in sends:
        if condition is None:
            copy.wait_send()
        else:
            pl.when(condition)(lambda copy=copy: copy.wait_send())


def group_size(slots):
    return max(size for size in range(1, 14) if slots % size == 0)


def reduce_blocks(rows, sizes):
    count = rows // 3
    return [(block * count, stage_plan(count, ("lat", "chan", "lon"), sizes)) for block in range(3)]


def finish_kernel(rows, kg_in, grad_out, kg_out, zeros, sems, kg_sems):
    zero_rows = zeros.shape[0]
    groups = rows.shape[0] // zero_rows
    in_ch = kg_in.shape[0] // 9
    writes = []
    for k in range(groups):
        at = pl.ds(k * zero_rows, zero_rows)
        writes.append(pltpu.make_async_copy(rows.at[at], grad_out.at[at, 0], sems.at[4 + 3 * k]))
    for block in range(3):
        for r in range(3):
            writes.append(
                pltpu.make_async_copy(
                    kg_in.at[pl.ds((3 * block + r) * in_ch, in_ch)],
                    kg_out.at[pl.ds((3 * r + TAP_ORDER[block]) * in_ch, in_ch)],
                    kg_sems.at[3 * block + r],
                )
            )
    for c in writes:
        c.start()
    zeros[...] = jnp.zeros(zeros.shape, BF16)
    for k in range(groups):
        at = pl.ds(k * zero_rows, zero_rows)
        writes.append(pltpu.make_async_copy(zeros, grad_out.at[at, 1], sems.at[3 + 3 * k]))
        writes[-1].start()
    for copy in writes:
        copy.wait()


def on_device(sizes, fine_act, coarse_grad, kernel):
    fine_rows, fine_cols, in_ch = fine_act.shape
    out_ch = kernel.shape[3]
    h, w = fine_rows // 2, fine_cols // 2
    lon_n, lat_n, chan_n = (sizes[a] for a in AXES)
    scale = 1.0 / math.sqrt(h * lat_n * chan_n * w * lon_n)
    cg = jnp.transpose(coarse_grad, (0, 2, 1))
    fine = fine_act.reshape(h, 2, fine_cols, in_ch)
    blocks = reduce_blocks(9 * in_ch, sizes)
    landing, count = [], 0
    groups = (h + 2) // group_size(h + 2)
    for block, stage in ((0, 0), (0, 1), (1, 0), (1, 1), (0, 2), (2, 0), (2, 1), (1, 2), (2, 2)):
        axis, part, _ = blocks[block][1][stage]
        landing.append(pltpu.VMEM((sizes[axis] - 1, part, out_ch), F32))
        count += sizes[axis] - 1
    dma = pltpu.SemaphoreType.DMA
    vmem = pl.BlockSpec(memory_space=pltpu.VMEM)
    hbm = pl.BlockSpec(memory_space=pltpu.HBM)
    rows, kg = pl.pallas_call(
        functools.partial(grads_kernel, sizes, h, w, out_ch, scale),
        out_shape=(
            pltpu.VMEM((h, fine_cols, in_ch), BF16),
            pltpu.VMEM((9 * in_ch, out_ch), F32),
        ),
        in_specs=[hbm, hbm, hbm],
        out_specs=(vmem, vmem),
        scratch_shapes=[
            pltpu.VMEM((h, fine_cols, in_ch), BF16),
            pltpu.VMEM((3, in_ch, 3 * out_ch), BF16),
            pltpu.VMEM((h + 2, out_ch, w), BF16),
            pltpu.VMEM((3 * out_ch, (h + 2) * LANES), BF16),
            pltpu.VMEM((in_ch, h * LANES), BF16),
            pltpu.VMEM((2, out_ch, LANES), BF16),
            pltpu.VMEM((2, out_ch, LANES), BF16),
            pltpu.VMEM((2, LANES, (h + 2) * LANES), BF16),
            pltpu.VMEM((9 * in_ch, out_ch), F32),
            dma((4,)),
            *landing,
            dma((10,)),
            dma((2 + groups,)),
            dma(((2 + groups) * (chan_n - 1) + 2,)),
            dma((2,)),
            dma((2,)),
            dma((count,)),
            dma((count,)),
            dma((count,)),
            dma((count,)),
        ],
        compiler_params=pltpu.CompilerParams(
            collective_id=0, has_side_effects=True, vmem_limit_bytes=60 * 1024 * 1024
        ),
        name="grads",
    )(fine, cg, kernel)
    zero_rows = math.gcd(h, 8)
    input_grad, kernel_grad = pl.pallas_call(
        finish_kernel,
        out_shape=(
            jax.ShapeDtypeStruct((h, 2, fine_cols, in_ch), BF16),
            jax.ShapeDtypeStruct(kg.shape, F32),
        ),
        in_specs=[vmem, vmem],
        out_specs=(hbm, hbm),
        scratch_shapes=[
            pltpu.VMEM((zero_rows, fine_cols, in_ch), BF16),
            dma((2 + 3 * (h // zero_rows),)),
            dma((9,)),
        ],
        compiler_params=pltpu.CompilerParams(vmem_limit_bytes=40 * 1024 * 1024),
        name="finish",
    )(rows, kg)
    return (input_grad.reshape(fine_act.shape), kernel_grad.reshape(3, 3, in_ch, out_ch))


def solution(mesh):
    placed = (P(("parts", "lat", "chan"), "lon", None), P(("parts", "lat"), "lon", "chan"), P())
    sizes = {axis: mesh.shape[axis] for axis in AXES}
    return jax.shard_map(
        functools.partial(on_device, sizes),
        mesh=mesh,
        in_specs=placed,
        out_specs=(P(("parts", "lat", "chan"), "lon", None), P("parts", None, None, None)),
        check_vma=False,
    )
```

```python
import functools
import math

import jax
import jax.numpy as jnp
from jax import lax
from jax.experimental import pallas as pl
from jax.experimental.pallas import tpu as pltpu
from jax.sharding import PartitionSpec as P

MESH = pl.DeviceIdType.MESH
LANES = 128
PACK = 16
F32 = jnp.float32
BF16 = jnp.bfloat16
AXES = ("lon", "lat", "chan")
VMEM_BYTES = 67043328


def one_hot(shape, test):
    rows = lax.broadcasted_iota(jnp.int32, shape, 0)
    cols = lax.broadcasted_iota(jnp.int32, shape, 1)
    return jnp.where(test(rows, cols), 1.0, 0.0).astype(BF16)


def share(rows, peers, unit):
    for size in range(unit, rows + 1, unit):
        if rows % size == 0 and rows // size <= peers:
            return size
    raise ValueError("no share")


class Plan:
    def __init__(self, sizes, fine_shape, cg_shape, kernel_shape):
        self.lon_n, self.lat_n, self.chan_n = (sizes[a] for a in AXES)
        self.h, self.w = fine_shape[0] // 2, fine_shape[1] // 2
        self.in_ch, self.out_ch = kernel_shape[2], kernel_shape[3]
        self.width = cg_shape[2]
        self.group = min(self.width, 32)
        self.units = self.width // self.group
        self.part = share(3 * self.group, self.lon_n, 8)
        self.owners = 3 * self.group // self.part
        self.cut = self.in_ch // self.lat_n
        self.fine_cuts = 4 if self.h % 4 == 0 else 1
        parcels = 3 + (self.chan_n - 1) * self.units
        self.remote = (
            2 + 2 + 2
            + (self.chan_n - 1) * (self.units + 1)
            + parcels * (self.lat_n + self.lon_n + 1)
            + self.units * (self.lon_n - 1)
            + self.units * self.lon_n * (self.chan_n - 1)
            + self.chan_n * self.units * (self.lat_n - 1)
        )


def grads_kernel(
    plan, scale,
    fine, cg, kernel, rows_out, kg_out,
    fbuf, kcat, tiles, xs, ev, tt, edge_out, edge_in, tedge_out, tedge_in,
    acc, land_lat, land_lon, land_x,
    fine_sem, kernel_sem, own_sem, halo_recv, send_sem, recv_sem,
):
    lon_n, lat_n, chan_n = plan.lon_n, plan.lat_n, plan.chan_n
    h, w, width, group, units = plan.h, plan.w, plan.width, plan.group, plan.units
    part, owners, out_ch, cut = plan.part, plan.owners, plan.out_ch, plan.cut
    sizes = {"lon": lon_n, "lat": lat_n, "chan": chan_n}
    me = {a: lax.axis_index(a) for a in AXES}
    lon, lat, chan = me["lon"], me["lat"], me["chan"]
    my_chunk = jnp.minimum(lon, owners - 1)
    is_owner = None if owners == lon_n else lon < owners

    def other(axis, step):
        return lax.rem(me[axis] + step + sizes[axis], sizes[axis])

    def channels(block, unit=0, size=None):
        start = pl.multiple_of(block * width + unit * group, PACK)
        return pl.ds(start, width if size is None else size)

    def guarded(condition, action):
        if condition is None:
            action()
        else:
            pl.when(condition)(action)

    step = h // plan.fine_cuts
    fine_in = []
    for k in range(plan.fine_cuts):
        at = pl.ds(k * step, step)
        fine_in.append(pltpu.make_async_copy(fine.at[at, 0], fbuf.at[at], fine_sem.at[k]))

    def first_row(p):
        return jnp.maximum(p * h - 1, 0), jnp.where(p > 0, 0, 1)

    own_from, own_to = first_row(chan)
    own_in = pltpu.make_async_copy(
        cg.at[pl.ds(own_from, h + 1)], tiles.at[pl.ds(own_to, h + 1), channels(chan)], own_sem.at[0]
    )
    inner = jnp.logical_and(chan > 0, chan < chan_n - 1)
    own_extra = pltpu.make_async_copy(
        cg.at[jnp.minimum((chan + 1) * h, chan_n * h - 1)], tiles.at[h + 1, channels(chan)], own_sem.at[1]
    )
    kernel_in = []
    for r in range(3):
        for s in range(3):
            n = 3 * r + s
            kernel_in.append(
                pltpu.make_async_copy(kernel.at[r, s], kcat.at[:, pl.ds(n * out_ch, out_ch)], kernel_sem.at[n])
            )
    barrier = pltpu.get_barrier_semaphore()
    greeted = 0
    for dl in range(lat_n):
        for dc in range(chan_n):
            if dl or dc:
                pl.semaphore_signal(
                    barrier, inc=1, device_id={"lat": other("lat", dl), "chan": other("chan", dc)}, device_id_type=MESH
                )
                greeted += 1
    for d in range(1, lon_n):
        pl.semaphore_signal(barrier, inc=1, device_id={"lon": other("lon", d)}, device_id_type=MESH)
        greeted += 1

    for copy in fine_in:
        copy.start()
    own_in.start()
    if chan_n > 2:
        pl.when(inner)(lambda: own_extra.start())
    for copy in kernel_in:
        copy.start()

    is_top = jnp.logical_and(lat == 0, chan == 0)
    is_bottom = jnp.logical_and(lat == lat_n - 1, chan == chan_n - 1)

    @pl.when(is_top)
    def _():
        tiles[0] = jnp.zeros(tiles.shape[1:], BF16)

    @pl.when(is_bottom)
    def _():
        tiles[h + 1] = jnp.zeros(tiles.shape[1:], BF16)

    def picked_column(row, col):
        s, j = row // LANES, row % LANES
        return jnp.logical_and(jnp.logical_and(col == 2 * (j + s - 1), j < w), col >= 0)

    pick = one_hot((3 * LANES, 2 * w), picked_column)

    def take_even(i, _):
        picked = jnp.dot(pick, fbuf[i], preferred_element_type=F32)
        at = pl.ds(pl.multiple_of(i * LANES, LANES), LANES)
        for s in range(3):
            ev[s, at, :] = picked[s * LANES:(s + 1) * LANES].astype(BF16)
        edge_out[0, pl.ds(i, 1), :] = picked[LANES + w - 1:LANES + w]
        edge_out[1, pl.ds(i, 1), :] = picked[LANES:LANES + 1]
        return 0

    for k in range(plan.fine_cuts):
        fine_in[k].wait()
        lax.fori_loop(k * step, (k + 1) * step, take_even, 0)

    pad = jnp.zeros((width, LANES - w), BF16) if w < LANES else None

    def fill(d, unit, size, which):
        at = pl.ds(d * width + unit * group, size)
        source = channels(other("chan", d), unit, size)
        for i in which:
            block = tiles[i, source, :]
            if pad is not None:
                block = jnp.concatenate([block, pad[:size]], axis=1)
            xs[at, pl.ds(i * LANES, LANES)] = block

    own_in.wait()
    if chan_n > 2:
        pl.when(inner)(lambda: own_extra.wait())
    fill(0, 0, width, range(1, h + 1))

    pl.semaphore_wait(barrier, greeted)

    sends = []

    def send(condition, src, dst, where, recv=None):
        n = len(sends)
        copy = pltpu.make_async_remote_copy(
            src_ref=src, dst_ref=dst, send_sem=send_sem.at[n], recv_sem=recv_sem.at[n] if recv is None else recv,
            device_id=where, device_id_type=MESH,
        )
        guarded(condition, lambda: copy.start())
        sends.append((condition, copy))
        return n

    def arrive(ref, n, condition=None):
        guarded(condition, lambda: pltpu.make_async_copy(ref, ref, recv_sem.at[n]).wait())

    def both(a, b):
        return b if a is None else a if b is None else jnp.logical_and(a, b)

    send(
        lat < lat_n - 1, cg.at[chan_n * h - 1], tiles.at[0, channels(chan)],
        {"lat": jnp.minimum(lat + 1, lat_n - 1), "chan": 0}, halo_recv.at[chan],
    )
    send(
        lat > 0, cg.at[0], tiles.at[h + 1, channels(chan)],
        {"lat": jnp.maximum(lat - 1, 0), "chan": chan_n - 1}, halo_recv.at[chan_n + chan],
    )
    edge_n = [
        send(None, edge_out.at[0], edge_in.at[0], {"lon": other("lon", 1)}),
        send(None, edge_out.at[1], edge_in.at[1], {"lon": other("lon", -1)}),
    ]
    tile_n = {}
    for d in range(1, chan_n):
        p = other("chan", -d)
        source, target = first_row(p)
        for u in range(units):
            tile_n[d, u] = send(
                None, cg.at[pl.ds(source, h + 1), pl.ds(u * group, group)],
                tiles.at[pl.ds(target, h + 1), channels(chan, u, group)], {"chan": p},
            )
        if chan_n > 2:
            tile_n[d] = send(
                jnp.logical_and(p > 0, p < chan_n - 1), cg.at[jnp.minimum((p + 1) * h, chan_n * h - 1)],
                tiles.at[h + 1, channels(chan)], {"chan": p},
            )

    def halo_arrive(d):
        block = other("chan", d)
        for row, n, condition in (
            (0, block, jnp.logical_and(chan == 0, lat > 0)),
            (h + 1, chan_n + block, jnp.logical_and(chan == chan_n - 1, lat < lat_n - 1)),
        ):
            ref = tiles.at[row, channels(block)]
            guarded(condition, lambda: pltpu.make_async_copy(ref, ref, halo_recv.at[n]).wait())

    def tiles_arrive(d, u):
        block = other("chan", d)
        _, target = first_row(chan)
        arrive(tiles.at[pl.ds(target, h + 1), channels(block, u, group)], tile_n[d, u])
        if u == 0:
            if chan_n > 2:
                arrive(tiles.at[h + 1, channels(block)], tile_n[d], inner)
            halo_arrive(d)

    def terms(d, first, count, s):
        pieces = []
        for u in range(first, first + count):
            for r in range(3):
                pieces.append(xs[pl.ds(d * width + u * group, group), pl.ds((2 - r) * LANES, h * LANES)])
        total = jnp.dot(jnp.concatenate(pieces, axis=0), ev[s], preferred_element_type=F32)
        for u in range(count):
            for k in range(owners):
                at = (u * owners + k) * part
                for half in range(lat_n):
                    acc[half, d * units + first + u, k, s] = total[at:at + part, half * cut:(half + 1) * cut]

    def lat_send(d, first, count, s0, s_n):
        g, s = pl.ds(d * units + first, count), pl.ds(s0, s_n)
        numbers = []
        for dl in range(1, lat_n):
            l = other("lat", dl)
            numbers.append(
                send(None, acc.at[l, g, :, s], land_lat.at[dl - 1, g, :, s], {"lat": l})
            )
        return numbers

    def lat_add(parcel, numbers):
        d, first, count, s0, s_n = parcel
        g, s = pl.ds(d * units + first, count), pl.ds(s0, s_n)
        for dl in range(1, lat_n):
            arrive(land_lat.at[dl - 1, g, :, s], numbers[dl - 1])
        total = acc[lat, g, :, s]
        for dl in range(1, lat_n):
            total = total + land_lat[dl - 1, g, :, s]
        acc[lat, g, :, s] = total
        result = []
        for dz in range(1, lon_n):
            k = other("lon", dz)
            result.append(
                send(
                    None if owners == lon_n else k < owners, acc.at[lat, g, jnp.minimum(k, owners - 1), s],
                    land_lon.at[dz - 1, g, s], {"lon": k},
                )
            )
        return result

    x_n = {}

    def lon_sum(parcel, numbers):
        d, first, count, s0, s_n = parcel
        g, s = pl.ds(d * units + first, count), pl.ds(s0, s_n)
        for dz in range(1, lon_n):
            arrive(land_lon.at[dz - 1, g, s], numbers[dz - 1], is_owner)
        total = acc[lat, g, my_chunk, s]
        for dz in range(1, lon_n):
            total = total + land_lon[dz - 1, g, s]
        return total

    def lon_add(parcel, numbers):
        d, first, count, s0, s_n = parcel
        g, s = pl.ds(d * units + first, count), pl.ds(s0, s_n)

        def add():
            acc[lat, g, my_chunk, s] = lon_sum(parcel, numbers)

        guarded(is_owner, add)
        x_n[parcel] = send(
            is_owner, acc.at[lat, g, my_chunk, s], land_x.at[d, pl.ds(first, count), s], {"chan": other("chan", d + 1)}
        )

    last = chan_n - 1
    mine = other("chan", last)
    z_n, fx_n, lat_n_of = {}, {}, {}

    def owner_of(dz):
        k = other("lon", -dz)
        return jnp.minimum(k, owners - 1), (None if owners == lon_n else k < owners)

    def forward(u, dz):
        k, there = owner_of(dz)
        at = kg_out.at[lat, mine, u, k]
        for e in range(1, chan_n):
            fx_n[u, dz, e] = send(there, at, at, {"chan": other("chan", e)})

    def finish(parcel, numbers):
        u = parcel[1]

        def add():
            total = lon_sum(parcel, numbers)
            for other_parcel, n in x_n.items():
                d, first, count, s0, s_n = other_parcel
                if first <= u < first + count and n not in done:
                    ref = land_x.at[d, pl.ds(first, count), pl.ds(s0, s_n)]
                    pltpu.make_async_copy(ref, ref, recv_sem.at[n]).wait()
                    done.append(n)
            total = total[0]
            for d in range(last):
                total = total + land_x[d, u]
            kg_out[lat, mine, u, my_chunk] = total * scale

        guarded(is_owner, add)
        at = kg_out.at[lat, mine, u, my_chunk]
        for dz in range(1, lon_n):
            z_n[u, dz] = send(is_owner, at, at, {"lon": other("lon", dz)})
        forward(u, 0)

    done = []

    def relay(u):
        for dz in range(1, lon_n):
            k, there = owner_of(dz)
            arrive(kg_out.at[lat, mine, u, k], z_n[u, dz], there)
            forward(u, dz)
        lat_forward(mine, u)

    def lat_forward(block, u):
        at = kg_out.at[lat, block, u]
        for dl in range(1, lat_n):
            n = send(None, at, at, {"lat": other("lat", dl)})
            lat_n_of[len(lat_n_of)] = (n, dl, block, u)

    def collect(u):
        for e in range(1, chan_n):
            block = other("chan", -e - 1)
            for dz in range(lon_n):
                k, there = owner_of(dz)
                arrive(kg_out.at[lat, block, u, k], fx_n[u, dz, e], there)
            lat_forward(block, u)

    def turned(row, col):
        s, j = row // w, row % w
        return col == j + 1 - s

    def make_taps():
        turn = one_hot((3 * w, w), turned)
        for i in range(0, h + 2, 2):
            pair = tiles[pl.ds(i, 2)].reshape(2 * out_ch, w)
            moved = lax.dot_general(turn, pair, (((1,), (1,)), ((), ())), preferred_element_type=F32)
            for k in range(2):
                lanes = slice(k * out_ch, (k + 1) * out_ch)
                for s in range(3):
                    tt[s, pl.ds((i + k) * w, w), :] = moved[s * w:(s + 1) * w, lanes].astype(BF16)
                tedge_out[0, pl.ds(i + k, 1), :] = moved[2 * w - 1:2 * w, lanes]
                tedge_out[1, pl.ds(i + k, 1), :] = moved[w:w + 1, lanes]

    def patch(buffer, base, row, value):
        start = base + row // PACK * PACK
        at = pl.ds(pl.multiple_of(start, PACK), PACK)
        old = buffer[at, :].astype(F32)
        rows = lax.broadcasted_iota(jnp.int32, old.shape, 0)
        buffer[at, :] = jnp.where(rows == row % PACK, value, old).astype(BF16)

    def patch_even(i, _):
        base = i * LANES
        patch(ev.at[0], base, 0, edge_in[0, pl.ds(i, 1), :])
        patch(ev.at[2], base, w - 1, edge_in[1, pl.ds(i, 1), :])
        return 0

    def patch_taps(i, _):
        base = i * w
        patch(tt.at[2], base, 0, tedge_in[0, pl.ds(i, 1), :])
        patch(tt.at[0], base, w - 1, tedge_in[1, pl.ds(i, 1), :])
        return 0

    ig_rows = math.gcd(h, 4)
    spread = one_hot((2 * w, w), lambda row, col: row == 2 * col)

    def even_grads(b, _):
        pieces = []
        for r in range(3):
            at = pl.ds(pl.multiple_of((b * ig_rows + 2 - r) * w, PACK), ig_rows * w)
            for s in range(3):
                pieces.append(tt[s, at, :])
        total = lax.dot_general(
            jnp.concatenate(pieces, axis=1), kcat[...], (((1,), (1,)), ((), ())), preferred_element_type=F32
        ).astype(BF16)
        for k in range(ig_rows):
            row = jnp.dot(spread, total[k * w:(k + 1) * w], preferred_element_type=F32)
            rows_out[b * ig_rows + k] = row.astype(BF16)
        return 0

    blocks = h // ig_rows
    state = {"ig": 0}

    def some_even_grads(count):
        end = min(blocks, state["ig"] + count)
        if end > state["ig"]:
            lax.fori_loop(state["ig"], end, even_grads, 0)
        state["ig"] = end

    halo_arrive(0)
    fill(0, 0, width, (0, h + 1))
    parcels = {}

    def begin(d, first, count, s0, s_n):
        parcel = (d, first, count, s0, s_n)
        for s in range(s0, s0 + s_n):
            terms(d, first, count, s)
        parcels[parcel] = lat_send(*parcel)
        return parcel

    a1 = begin(0, 0, units, 1, 1)
    for n, ref in zip(edge_n, (edge_in.at[0], edge_in.at[1])):
        arrive(ref, n)
    lax.fori_loop(0, h, patch_even, 0)
    parcels[a1] = lat_add(a1, parcels[a1])
    a0 = begin(0, 0, units, 0, 1)
    a2 = begin(0, 0, units, 2, 1)
    parcels[a0] = lat_add(a0, parcels[a0])
    parcels[a2] = lat_add(a2, parcels[a2])
    own = [a1, a0, a2]
    early = []
    for d in range(1, chan_n):
        for u in range(units):
            tiles_arrive(d, u)
            fill(d, u, group, range(h + 2))
            parcel = begin(d, u, 1, 0, 3)
            early.append(parcel)
            parcels[parcel] = lat_add(parcel, parcels[parcel])
    for parcel in own + [q for q in early if q[0] < last]:
        lon_add(parcel, parcels[parcel])
    make_taps()
    tedge_n = [
        send(None, tedge_out.at[0], tedge_in.at[0], {"lon": other("lon", 1)}),
        send(None, tedge_out.at[1], tedge_in.at[1], {"lon": other("lon", -1)}),
    ]
    finals = [q for q in early if q[0] == last]
    for copy in kernel_in:
        copy.wait()
    for n, ref in zip(tedge_n, (tedge_in.at[0], tedge_in.at[1])):
        arrive(ref, n)
    lax.fori_loop(0, h + 2, patch_taps, 0)
    for k, parcel in enumerate(finals):
        finish(parcel, parcels[parcel])
        some_even_grads(blocks // (2 * len(finals)))
    for k, parcel in enumerate(finals):
        relay(parcel[1])
        some_even_grads(-(-blocks // (2 * len(finals))))
    some_even_grads(blocks)
    for parcel in finals:
        collect(parcel[1])
    for n, dl, block, u in lat_n_of.values():
        there = other("lat", -dl)
        arrive(kg_out.at[there, block, u], n)
    for condition, copy in sends:
        guarded(condition, lambda: copy.wait_send())


def finish_kernel(plan, rows, kg_in, grad_out, kg_out, zeros, turned, sems, kg_sems):
    zero_rows = zeros.shape[0]
    groups = rows.shape[0] // zero_rows
    in_ch, part, group, cut = plan.in_ch, plan.part, plan.group, plan.cut
    writes = []
    for k in range(groups):
        at = pl.ds(k * zero_rows, zero_rows)
        writes.append(pltpu.make_async_copy(rows.at[at], grad_out.at[at, 0], sems.at[2 * k]))
        writes[-1].start()
    zeros[...] = jnp.zeros(zeros.shape, BF16)
    for k in range(groups):
        at = pl.ds(k * zero_rows, zero_rows)
        writes.append(pltpu.make_async_copy(zeros, grad_out.at[at, 1], sems.at[2 * k + 1]))
        writes[-1].start()
    for s in range(3):
        for half in range(plan.lat_n):
            pieces = [[], [], []]
            for p in range(plan.chan_n):
                for u in range(plan.units):
                    stack = jnp.concatenate([kg_in[half, p, u, k, s] for k in range(plan.owners)], axis=0)
                    for r in range(3):
                        pieces[r].append(stack[r * group:(r + 1) * group])
            for r in range(3):
                turned[3 * r + s, pl.ds(half * cut, cut), :] = jnp.concatenate(pieces[r], axis=0).T
        for r in range(3):
            n = 3 * r + s
            writes.append(
                pltpu.make_async_copy(turned.at[n], kg_out.at[pl.ds(n * in_ch, in_ch)], kg_sems.at[n])
            )
            writes[-1].start()
    for copy in writes:
        copy.wait()


def on_device(sizes, fine_act, coarse_grad, kernel):
    plan = Plan(sizes, fine_act.shape, coarse_grad.shape, kernel.shape)
    fine_rows, fine_cols, in_ch = fine_act.shape
    h, w, out_ch = plan.h, plan.w, plan.out_ch
    scale = 1.0 / math.sqrt(h * plan.lat_n * plan.chan_n * w * plan.lon_n)
    cg = jnp.transpose(coarse_grad, (0, 2, 1))
    fine = fine_act.reshape(h, 2, fine_cols, in_ch)
    dma = pltpu.SemaphoreType.DMA
    vmem = pl.BlockSpec(memory_space=pltpu.VMEM)
    hbm = pl.BlockSpec(memory_space=pltpu.HBM)
    sums = plan.chan_n * plan.units
    chunk = (3, plan.part, plan.cut)
    rows_shape = (h, fine_cols, in_ch)
    kg_shape = (plan.lat_n, plan.chan_n, plan.units, plan.owners) + chunk
    edge_rows = -(-(h + 2) // 8) * 8
    held = 2 * math.prod(rows_shape) + 4 * math.prod(kg_shape)
    rows, kg = pl.pallas_call(
        functools.partial(grads_kernel, plan, scale),
        out_shape=(pltpu.VMEM(rows_shape, BF16), pltpu.VMEM(kg_shape, F32)),
        in_specs=[hbm, hbm, hbm],
        out_specs=(vmem, vmem),
        scratch_shapes=[
            pltpu.VMEM((h, fine_cols, in_ch), BF16),
            pltpu.VMEM((in_ch, 9 * out_ch), BF16),
            pltpu.VMEM((h + 2, out_ch, w), BF16),
            pltpu.VMEM((out_ch, (h + 2) * LANES), BF16),
            pltpu.VMEM((3, h * LANES, in_ch), BF16),
            pltpu.VMEM((3, (h + 2) * w, out_ch), BF16),
            pltpu.VMEM((2, edge_rows, in_ch), F32),
            pltpu.VMEM((2, edge_rows, in_ch), F32),
            pltpu.VMEM((2, edge_rows, out_ch), F32),
            pltpu.VMEM((2, edge_rows, out_ch), F32),
            pltpu.VMEM((plan.lat_n, sums, plan.owners) + chunk, F32),
            pltpu.VMEM((plan.lat_n - 1, sums, plan.owners) + chunk, F32),
            pltpu.VMEM((plan.lon_n - 1, sums) + chunk, F32),
            pltpu.VMEM((plan.chan_n - 1, plan.units) + chunk, F32),
            dma((plan.fine_cuts,)),
            dma((9,)),
            dma((2,)),
            dma((2 * plan.chan_n,)),
            dma((plan.remote,)),
            dma((plan.remote,)),
        ],
        compiler_params=pltpu.CompilerParams(
            collective_id=0, has_side_effects=True, vmem_limit_bytes=(VMEM_BYTES - held) // 65536 * 65536
        ),
        name="grads",
    )(fine, cg, kernel)
    zero_rows = math.gcd(h, 8)
    input_grad, kernel_grad = pl.pallas_call(
        functools.partial(finish_kernel, plan),
        out_shape=(
            jax.ShapeDtypeStruct((h, 2, fine_cols, in_ch), BF16),
            jax.ShapeDtypeStruct((9 * in_ch, out_ch), F32),
        ),
        in_specs=[vmem, vmem],
        out_specs=(hbm, hbm),
        scratch_shapes=[
            pltpu.VMEM((zero_rows, fine_cols, in_ch), BF16),
            pltpu.VMEM((9, in_ch, out_ch), F32),
            dma((2 * (h // zero_rows),)),
            dma((9,)),
        ],
        compiler_params=pltpu.CompilerParams(vmem_limit_bytes=VMEM_BYTES // 4),
        name="finish",
    )(rows, kg)
    return (input_grad.reshape(fine_act.shape), kernel_grad.reshape(3, 3, in_ch, out_ch))


def solution(mesh):
    placed = (P(("parts", "lat", "chan"), "lon", None), P(("parts", "lat"), "lon", "chan"), P())
    sizes = {axis: mesh.shape[axis] for axis in AXES}
    return jax.shard_map(
        functools.partial(on_device, sizes),
        mesh=mesh,
        in_specs=placed,
        out_specs=(P(("parts", "lat", "chan"), "lon", None), P("parts", None, None, None)),
        check_vma=False,
    )
```

```python
import functools
import math

import jax
import jax.numpy as jnp
from jax import lax
from jax.experimental import pallas as pl
from jax.experimental.pallas import tpu as pltpu
from jax.sharding import PartitionSpec as P

MESH = pl.DeviceIdType.MESH
LANES = 128
PACK = 16
F32 = jnp.float32
BF16 = jnp.bfloat16
AXES = ("lon", "lat", "chan")
VMEM_BYTES = 67043328
EARLY_CUTS = 1


def one_hot(shape, test):
    rows = lax.broadcasted_iota(jnp.int32, shape, 0)
    cols = lax.broadcasted_iota(jnp.int32, shape, 1)
    return jnp.where(test(rows, cols), 1.0, 0.0).astype(BF16)


def share(rows, peers, unit):
    for size in range(unit, rows + 1, unit):
        if rows % size == 0 and rows // size <= peers:
            return size
    raise ValueError("no share")


class Plan:
    def __init__(self, sizes, fine_shape, cg_shape, kernel_shape):
        self.lon_n, self.lat_n, self.chan_n = (sizes[a] for a in AXES)
        self.h, self.w = fine_shape[0] // 2, fine_shape[1] // 2
        self.in_ch, self.out_ch = kernel_shape[2], kernel_shape[3]
        self.width = cg_shape[2]
        self.group = min(self.width, 32)
        self.units = self.width // self.group
        self.part = share(3 * self.group, self.lon_n, 8)
        self.owners = 3 * self.group // self.part
        self.cut = self.in_ch // self.lat_n
        self.fine_cuts = 4 if self.h % 4 == 0 else 1
        parcels = 3 + (self.chan_n - 1) * self.units
        self.remote = (
            2 + 2 + 2
            + (self.chan_n - 1) * (self.units + 1)
            + parcels * (self.lat_n + self.lon_n + 1)
            + self.units * (self.lon_n - 1)
            + self.units * self.lon_n * (self.chan_n - 1)
            + self.chan_n * self.units * (self.lat_n - 1)
        )


def grads_kernel(
    plan, scale,
    fine, cg, kernel, rows_out, kg_out,
    fbuf, kcat, tiles, xs, ev, tt, edge_out, edge_in, tedge_out, tedge_in,
    acc, land_lat, land_lon, land_x,
    fine_sem, kernel_sem, own_sem, halo_recv, send_sem, recv_sem,
):
    lon_n, lat_n, chan_n = plan.lon_n, plan.lat_n, plan.chan_n
    h, w, width, group, units = plan.h, plan.w, plan.width, plan.group, plan.units
    part, owners, out_ch, cut = plan.part, plan.owners, plan.out_ch, plan.cut
    sizes = {"lon": lon_n, "lat": lat_n, "chan": chan_n}
    me = {a: lax.axis_index(a) for a in AXES}
    lon, lat, chan = me["lon"], me["lat"], me["chan"]
    my_chunk = jnp.minimum(lon, owners - 1)
    is_owner = None if owners == lon_n else lon < owners

    def other(axis, step):
        return lax.rem(me[axis] + step + sizes[axis], sizes[axis])

    def channels(block, unit=0, size=None):
        start = pl.multiple_of(block * width + unit * group, PACK)
        return pl.ds(start, width if size is None else size)

    def guarded(condition, action):
        if condition is None:
            action()
        else:
            pl.when(condition)(action)

    step = h // plan.fine_cuts
    fine_in = []
    for k in range(plan.fine_cuts):
        at = pl.ds(k * step, step)
        fine_in.append(pltpu.make_async_copy(fine.at[at, 0], fbuf.at[at], fine_sem.at[k]))

    def first_row(p):
        return jnp.maximum(p * h - 1, 0), jnp.where(p > 0, 0, 1)

    own_from, own_to = first_row(chan)
    own_in = pltpu.make_async_copy(
        cg.at[pl.ds(own_from, h + 1)], tiles.at[pl.ds(own_to, h + 1), channels(chan)], own_sem.at[0]
    )
    inner = jnp.logical_and(chan > 0, chan < chan_n - 1)
    own_extra = pltpu.make_async_copy(
        cg.at[jnp.minimum((chan + 1) * h, chan_n * h - 1)], tiles.at[h + 1, channels(chan)], own_sem.at[1]
    )
    kernel_in = []
    for r in range(3):
        for s in range(3):
            n = 3 * r + s
            kernel_in.append(
                pltpu.make_async_copy(kernel.at[r, s], kcat.at[:, pl.ds(n * out_ch, out_ch)], kernel_sem.at[n])
            )
    barrier = pltpu.get_barrier_semaphore()
    greeted = 0
    for dl in range(lat_n):
        for dc in range(chan_n):
            if dl or dc:
                pl.semaphore_signal(
                    barrier, inc=1, device_id={"lat": other("lat", dl), "chan": other("chan", dc)}, device_id_type=MESH
                )
                greeted += 1
    for d in range(1, lon_n):
        pl.semaphore_signal(barrier, inc=1, device_id={"lon": other("lon", d)}, device_id_type=MESH)
        greeted += 1

    for copy in fine_in:
        copy.start()
    own_in.start()
    if chan_n > 2:
        pl.when(inner)(lambda: own_extra.start())
    for copy in kernel_in:
        copy.start()

    is_top = jnp.logical_and(lat == 0, chan == 0)
    is_bottom = jnp.logical_and(lat == lat_n - 1, chan == chan_n - 1)

    @pl.when(is_top)
    def _():
        tiles[0] = jnp.zeros(tiles.shape[1:], BF16)

    @pl.when(is_bottom)
    def _():
        tiles[h + 1] = jnp.zeros(tiles.shape[1:], BF16)

    def picked_column(row, col):
        s, j = row // LANES, row % LANES
        return jnp.logical_and(jnp.logical_and(col == 2 * (j + s - 1), j < w), col >= 0)

    pick = one_hot((3 * LANES, 2 * w), picked_column)

    def take_even(i, _):
        picked = jnp.dot(pick, fbuf[i], preferred_element_type=F32)
        at = pl.ds(pl.multiple_of(i * LANES, LANES), LANES)
        for s in range(3):
            ev[s, at, :] = picked[s * LANES:(s + 1) * LANES].astype(BF16)
        return 0

    def take_edges(rows):
        for i in rows:
            edge_out[1, pl.ds(i, 1), :] = fbuf[i, pl.ds(0, PACK), :].astype(F32)[0:1]
            edge_out[0, pl.ds(i, 1), :] = fbuf[i, pl.ds(2 * w - PACK, PACK), :].astype(F32)[PACK - 2:PACK - 1]

    def take_evens(cuts):
        for k in cuts:
            lax.fori_loop(k * step, (k + 1) * step, take_even, 0, unroll=2 - step % 2)

    for k in range(plan.fine_cuts):
        fine_in[k].wait()
        take_edges(range(k * step, (k + 1) * step))
    take_evens(range(EARLY_CUTS))

    pad = jnp.zeros((width, LANES - w), BF16) if w < LANES else None

    def fill(d, unit, size, which):
        at = pl.ds(d * width + unit * group, size)
        source = channels(other("chan", d), unit, size)
        for i in which:
            block = tiles[i, source, :]
            if pad is not None:
                block = jnp.concatenate([block, pad[:size]], axis=1)
            xs[at, pl.ds(i * LANES, LANES)] = block

    pl.semaphore_wait(barrier, greeted)

    sends = []

    def send(condition, src, dst, where, recv=None):
        n = len(sends)
        copy = pltpu.make_async_remote_copy(
            src_ref=src, dst_ref=dst, send_sem=send_sem.at[n], recv_sem=recv_sem.at[n] if recv is None else recv,
            device_id=where, device_id_type=MESH,
        )
        guarded(condition, lambda: copy.start())
        sends.append((condition, copy))
        return n

    def arrive(ref, n, condition=None):
        guarded(condition, lambda: pltpu.make_async_copy(ref, ref, recv_sem.at[n]).wait())

    def both(a, b):
        return b if a is None else a if b is None else jnp.logical_and(a, b)

    send(
        lat < lat_n - 1, cg.at[chan_n * h - 1], tiles.at[0, channels(chan)],
        {"lat": jnp.minimum(lat + 1, lat_n - 1), "chan": 0}, halo_recv.at[chan],
    )
    send(
        lat > 0, cg.at[0], tiles.at[h + 1, channels(chan)],
        {"lat": jnp.maximum(lat - 1, 0), "chan": chan_n - 1}, halo_recv.at[chan_n + chan],
    )
    edge_n = [
        send(None, edge_out.at[0], edge_in.at[0], {"lon": other("lon", 1)}),
        send(None, edge_out.at[1], edge_in.at[1], {"lon": other("lon", -1)}),
    ]
    tile_n = {}
    for d in range(1, chan_n):
        p = other("chan", -d)
        source, target = first_row(p)
        for u in range(units):
            tile_n[d, u] = send(
                None, cg.at[pl.ds(source, h + 1), pl.ds(u * group, group)],
                tiles.at[pl.ds(target, h + 1), channels(chan, u, group)], {"chan": p},
            )
        if chan_n > 2:
            tile_n[d] = send(
                jnp.logical_and(p > 0, p < chan_n - 1), cg.at[jnp.minimum((p + 1) * h, chan_n * h - 1)],
                tiles.at[h + 1, channels(chan)], {"chan": p},
            )

    def halo_arrive(d):
        block = other("chan", d)
        for row, n, condition in (
            (0, block, jnp.logical_and(chan == 0, lat > 0)),
            (h + 1, chan_n + block, jnp.logical_and(chan == chan_n - 1, lat < lat_n - 1)),
        ):
            ref = tiles.at[row, channels(block)]
            guarded(condition, lambda: pltpu.make_async_copy(ref, ref, halo_recv.at[n]).wait())

    def tiles_arrive(d, u):
        block = other("chan", d)
        _, target = first_row(chan)
        arrive(tiles.at[pl.ds(target, h + 1), channels(block, u, group)], tile_n[d, u])
        if u == 0:
            if chan_n > 2:
                arrive(tiles.at[h + 1, channels(block)], tile_n[d], inner)
            halo_arrive(d)

    def terms(d, first, count, s):
        pieces = []
        for u in range(first, first + count):
            for r in range(3):
                pieces.append(xs[pl.ds(d * width + u * group, group), pl.ds((2 - r) * LANES, h * LANES)])
        total = jnp.dot(jnp.concatenate(pieces, axis=0), ev[s], preferred_element_type=F32)
        for u in range(count):
            for k in range(owners):
                at = (u * owners + k) * part
                for half in range(lat_n):
                    acc[half, d * units + first + u, k, s] = total[at:at + part, half * cut:(half + 1) * cut]

    def lat_send(d, first, count, s0, s_n):
        g, s = pl.ds(d * units + first, count), pl.ds(s0, s_n)
        numbers = []
        for dl in range(1, lat_n):
            l = other("lat", dl)
            numbers.append(
                send(None, acc.at[l, g, :, s], land_lat.at[dl - 1, g, :, s], {"lat": l})
            )
        return numbers

    def lat_add(parcel, numbers):
        d, first, count, s0, s_n = parcel
        g, s = pl.ds(d * units + first, count), pl.ds(s0, s_n)
        for dl in range(1, lat_n):
            arrive(land_lat.at[dl - 1, g, :, s], numbers[dl - 1])
        total = acc[lat, g, :, s]
        for dl in range(1, lat_n):
            total = total + land_lat[dl - 1, g, :, s]
        acc[lat, g, :, s] = total
        result = []
        for dz in range(1, lon_n):
            k = other("lon", dz)
            result.append(
                send(
                    None if owners == lon_n else k < owners, acc.at[lat, g, jnp.minimum(k, owners - 1), s],
                    land_lon.at[dz - 1, g, s], {"lon": k},
                )
            )
        return result

    x_n = {}

    def lon_sum(parcel, numbers):
        d, first, count, s0, s_n = parcel
        g, s = pl.ds(d * units + first, count), pl.ds(s0, s_n)
        for dz in range(1, lon_n):
            arrive(land_lon.at[dz - 1, g, s], numbers[dz - 1], is_owner)
        total = acc[lat, g, my_chunk, s]
        for dz in range(1, lon_n):
            total = total + land_lon[dz - 1, g, s]
        return total

    def lon_add(parcel, numbers):
        d, first, count, s0, s_n = parcel
        g, s = pl.ds(d * units + first, count), pl.ds(s0, s_n)

        def add():
            acc[lat, g, my_chunk, s] = lon_sum(parcel, numbers)

        guarded(is_owner, add)
        x_n[parcel] = send(
            is_owner, acc.at[lat, g, my_chunk, s], land_x.at[d, pl.ds(first, count), s], {"chan": other("chan", d + 1)}
        )

    last = chan_n - 1
    mine = other("chan", last)
    z_n, fx_n, lat_n_of = {}, {}, {}

    def owner_of(dz):
        k = other("lon", -dz)
        return jnp.minimum(k, owners - 1), (None if owners == lon_n else k < owners)

    def forward(u, dz):
        k, there = owner_of(dz)
        at = kg_out.at[lat, mine, u, k]
        for e in range(1, chan_n):
            fx_n[u, dz, e] = send(there, at, at, {"chan": other("chan", e)})

    def finish(parcel, numbers):
        u = parcel[1]

        def add():
            total = lon_sum(parcel, numbers)
            for other_parcel, n in x_n.items():
                d, first, count, s0, s_n = other_parcel
                if first <= u < first + count and n not in done:
                    ref = land_x.at[d, pl.ds(first, count), pl.ds(s0, s_n)]
                    pltpu.make_async_copy(ref, ref, recv_sem.at[n]).wait()
                    done.append(n)
            total = total[0]
            for d in range(last):
                total = total + land_x[d, u]
            kg_out[lat, mine, u, my_chunk] = total * scale

        guarded(is_owner, add)
        at = kg_out.at[lat, mine, u, my_chunk]
        for dz in range(1, lon_n):
            z_n[u, dz] = send(is_owner, at, at, {"lon": other("lon", dz)})
        forward(u, 0)

    done = []

    def relay(u):
        for dz in range(1, lon_n):
            k, there = owner_of(dz)
            arrive(kg_out.at[lat, mine, u, k], z_n[u, dz], there)
            forward(u, dz)
        lat_forward(mine, u)

    def lat_forward(block, u):
        at = kg_out.at[lat, block, u]
        for dl in range(1, lat_n):
            n = send(None, at, at, {"lat": other("lat", dl)})
            lat_n_of[len(lat_n_of)] = (n, dl, block, u)

    def collect(u):
        for e in range(1, chan_n):
            block = other("chan", -e - 1)
            for dz in range(lon_n):
                k, there = owner_of(dz)
                arrive(kg_out.at[lat, block, u, k], fx_n[u, dz, e], there)
            lat_forward(block, u)

    def turned(row, col):
        s, j = row // w, row % w
        return col == j + 1 - s

    def make_taps():
        turn = one_hot((3 * w, w), turned)
        for i in range(0, h + 2, 2):
            pair = tiles[pl.ds(i, 2)].reshape(2 * out_ch, w)
            moved = lax.dot_general(turn, pair, (((1,), (1,)), ((), ())), preferred_element_type=F32)
            for k in range(2):
                lanes = slice(k * out_ch, (k + 1) * out_ch)
                for s in range(3):
                    tt[s, pl.ds((i + k) * w, w), :] = moved[s * w:(s + 1) * w, lanes].astype(BF16)
                tedge_out[0, pl.ds(i + k, 1), :] = moved[2 * w - 1:2 * w, lanes]
                tedge_out[1, pl.ds(i + k, 1), :] = moved[w:w + 1, lanes]

    def patch(buffer, base, row, value):
        start = base + row // PACK * PACK
        at = pl.ds(start, PACK)
        old = buffer[at, :].astype(F32)
        rows = lax.broadcasted_iota(jnp.int32, old.shape, 0)
        buffer[at, :] = jnp.where(rows == row % PACK, value, old).astype(BF16)

    def patch_even(i):
        base = i * LANES
        patch(ev.at[0], base, 0, edge_in[0, pl.ds(i, 1), :])
        patch(ev.at[2], base, w - 1, edge_in[1, pl.ds(i, 1), :])

    def patch_taps(i):
        base = i * w
        patch(tt.at[2], base, 0, tedge_in[0, pl.ds(i, 1), :])
        patch(tt.at[0], base, w - 1, tedge_in[1, pl.ds(i, 1), :])

    ig_rows = math.gcd(h, 4)
    spread = one_hot((2 * w, w), lambda row, col: row == 2 * col)

    def even_grads(b, _):
        pieces = []
        for r in range(3):
            at = pl.ds(pl.multiple_of((b * ig_rows + 2 - r) * w, PACK), ig_rows * w)
            for s in range(3):
                pieces.append(tt[s, at, :])
        total = lax.dot_general(
            jnp.concatenate(pieces, axis=1), kcat[...], (((1,), (1,)), ((), ())), preferred_element_type=F32
        ).astype(BF16)
        for k in range(ig_rows):
            row = jnp.dot(spread, total[k * w:(k + 1) * w], preferred_element_type=F32)
            rows_out[b * ig_rows + k] = row.astype(BF16)
        return 0

    blocks = h // ig_rows
    state = {"ig": 0}

    def some_even_grads(count):
        end = min(blocks, state["ig"] + count)
        if end > state["ig"]:
            lax.fori_loop(state["ig"], end, even_grads, 0)
        state["ig"] = end

    take_evens(range(EARLY_CUTS, plan.fine_cuts))
    own_in.wait()
    if chan_n > 2:
        pl.when(inner)(lambda: own_extra.wait())
    halo_arrive(0)
    fill(0, 0, width, range(h + 2))
    parcels = {}

    def begin(d, first, count, s0, s_n):
        parcel = (d, first, count, s0, s_n)
        for s in range(s0, s0 + s_n):
            terms(d, first, count, s)
        parcels[parcel] = lat_send(*parcel)
        return parcel

    a1 = begin(0, 0, units, 1, 1)
    for n, ref in zip(edge_n, (edge_in.at[0], edge_in.at[1])):
        arrive(ref, n)
    for i in range(h):
        patch_even(i)
    parcels[a1] = lat_add(a1, parcels[a1])
    a0 = begin(0, 0, units, 0, 1)
    a2 = begin(0, 0, units, 2, 1)
    parcels[a0] = lat_add(a0, parcels[a0])
    parcels[a2] = lat_add(a2, parcels[a2])
    own = [a1, a0, a2]
    early = []
    for d in range(1, chan_n):
        for u in range(units):
            tiles_arrive(d, u)
            fill(d, u, group, range(h + 2))
            parcel = begin(d, u, 1, 0, 3)
            early.append(parcel)
            parcels[parcel] = lat_add(parcel, parcels[parcel])
    finals = [q for q in early if q[0] == last]
    for parcel in own + early[:-len(finals)]:
        lon_add(parcel, parcels[parcel])
    make_taps()
    tedge_n = [
        send(None, tedge_out.at[0], tedge_in.at[0], {"lon": other("lon", 1)}),
        send(None, tedge_out.at[1], tedge_in.at[1], {"lon": other("lon", -1)}),
    ]
    for copy in kernel_in:
        copy.wait()
    for parcel in finals:
        finish(parcel, parcels[parcel])
    for n, ref in zip(tedge_n, (tedge_in.at[0], tedge_in.at[1])):
        arrive(ref, n)
    for i in range(h + 2):
        patch_taps(i)
    for parcel in finals[:-1]:
        relay(parcel[1])
    some_even_grads(3)
    relay(finals[-1][1])
    some_even_grads(9)
    for parcel in finals:
        collect(parcel[1])
    for n, dl, block, u in lat_n_of.values():
        there = other("lat", -dl)
        arrive(kg_out.at[there, block, u], n)
    for condition, copy in sends:
        guarded(condition, lambda: copy.wait_send())


def finish_kernel(plan, rows, kg_in, grad_out, kg_out, zeros, turned, sems, kg_sems):
    zero_rows = zeros.shape[0]
    groups = rows.shape[0] // zero_rows
    in_ch, part, group, cut = plan.in_ch, plan.part, plan.group, plan.cut
    writes = []
    for k in range(groups):
        at = pl.ds(k * zero_rows, zero_rows)
        writes.append(pltpu.make_async_copy(rows.at[at], grad_out.at[at, 0], sems.at[2 * k]))
        writes[-1].start()
    zeros[...] = jnp.zeros(zeros.shape, BF16)
    for k in range(groups):
        at = pl.ds(k * zero_rows, zero_rows)
        writes.append(pltpu.make_async_copy(zeros, grad_out.at[at, 1], sems.at[2 * k + 1]))
        writes[-1].start()
    for s in range(3):
        for half in range(plan.lat_n):
            pieces = [[], [], []]
            for p in range(plan.chan_n):
                for u in range(plan.units):
                    stack = jnp.concatenate([kg_in[half, p, u, k, s] for k in range(plan.owners)], axis=0)
                    for r in range(3):
                        pieces[r].append(stack[r * group:(r + 1) * group])
            for r in range(3):
                turned[3 * r + s, pl.ds(half * cut, cut), :] = jnp.concatenate(pieces[r], axis=0).T
        for r in range(3):
            n = 3 * r + s
            writes.append(
                pltpu.make_async_copy(turned.at[n], kg_out.at[pl.ds(n * in_ch, in_ch)], kg_sems.at[n])
            )
            writes[-1].start()
    for copy in writes:
        copy.wait()


def on_device(sizes, fine_act, coarse_grad, kernel):
    plan = Plan(sizes, fine_act.shape, coarse_grad.shape, kernel.shape)
    fine_rows, fine_cols, in_ch = fine_act.shape
    h, w, out_ch = plan.h, plan.w, plan.out_ch
    scale = 1.0 / math.sqrt(h * plan.lat_n * plan.chan_n * w * plan.lon_n)
    cg = jnp.transpose(coarse_grad, (0, 2, 1))
    fine = fine_act.reshape(h, 2, fine_cols, in_ch)
    dma = pltpu.SemaphoreType.DMA
    vmem = pl.BlockSpec(memory_space=pltpu.VMEM)
    hbm = pl.BlockSpec(memory_space=pltpu.HBM)
    sums = plan.chan_n * plan.units
    chunk = (3, plan.part, plan.cut)
    rows_shape = (h, fine_cols, in_ch)
    kg_shape = (plan.lat_n, plan.chan_n, plan.units, plan.owners) + chunk
    edge_rows = -(-(h + 2) // 8) * 8
    held = 2 * math.prod(rows_shape) + 4 * math.prod(kg_shape)
    rows, kg = pl.pallas_call(
        functools.partial(grads_kernel, plan, scale),
        out_shape=(pltpu.VMEM(rows_shape, BF16), pltpu.VMEM(kg_shape, F32)),
        in_specs=[hbm, hbm, hbm],
        out_specs=(vmem, vmem),
        scratch_shapes=[
            pltpu.VMEM((h, fine_cols, in_ch), BF16),
            pltpu.VMEM((in_ch, 9 * out_ch), BF16),
            pltpu.VMEM((h + 2, out_ch, w), BF16),
            pltpu.VMEM((out_ch, (h + 2) * LANES), BF16),
            pltpu.VMEM((3, h * LANES, in_ch), BF16),
            pltpu.VMEM((3, (h + 2) * w, out_ch), BF16),
            pltpu.VMEM((2, edge_rows, in_ch), F32),
            pltpu.VMEM((2, edge_rows, in_ch), F32),
            pltpu.VMEM((2, edge_rows, out_ch), F32),
            pltpu.VMEM((2, edge_rows, out_ch), F32),
            pltpu.VMEM((plan.lat_n, sums, plan.owners) + chunk, F32),
            pltpu.VMEM((plan.lat_n - 1, sums, plan.owners) + chunk, F32),
            pltpu.VMEM((plan.lon_n - 1, sums) + chunk, F32),
            pltpu.VMEM((plan.chan_n - 1, plan.units) + chunk, F32),
            dma((plan.fine_cuts,)),
            dma((9,)),
            dma((2,)),
            dma((2 * plan.chan_n,)),
            dma((plan.remote,)),
            dma((plan.remote,)),
        ],
        compiler_params=pltpu.CompilerParams(
            collective_id=0, has_side_effects=True, vmem_limit_bytes=(VMEM_BYTES - held) // 65536 * 65536
        ),
        name="grads",
    )(fine, cg, kernel)
    zero_rows = math.gcd(h, 8)
    input_grad, kernel_grad = pl.pallas_call(
        functools.partial(finish_kernel, plan),
        out_shape=(
            jax.ShapeDtypeStruct((h, 2, fine_cols, in_ch), BF16),
            jax.ShapeDtypeStruct((9 * in_ch, out_ch), F32),
        ),
        in_specs=[vmem, vmem],
        out_specs=(hbm, hbm),
        scratch_shapes=[
            pltpu.VMEM((zero_rows, fine_cols, in_ch), BF16),
            pltpu.VMEM((9, in_ch, out_ch), F32),
            dma((2 * (h // zero_rows),)),
            dma((9,)),
        ],
        compiler_params=pltpu.CompilerParams(vmem_limit_bytes=VMEM_BYTES // 4),
        name="finish",
    )(rows, kg)
    return (input_grad.reshape(fine_act.shape), kernel_grad.reshape(3, 3, in_ch, out_ch))


def solution(mesh):
    placed = (P(("parts", "lat", "chan"), "lon", None), P(("parts", "lat"), "lon", "chan"), P())
    sizes = {axis: mesh.shape[axis] for axis in AXES}
    return jax.shard_map(
        functools.partial(on_device, sizes),
        mesh=mesh,
        in_specs=placed,
        out_specs=(P(("parts", "lat", "chan"), "lon", None), P("parts", None, None, None)),
        check_vma=False,
    )
```

```python
import functools
import math

import jax
import jax.numpy as jnp
from jax import lax
from jax.experimental import pallas as pl
from jax.experimental.pallas import tpu as pltpu
from jax.sharding import PartitionSpec as P

MESH = pl.DeviceIdType.MESH
LANES = 128
PACK = 16
F32 = jnp.float32
BF16 = jnp.bfloat16
AXES = ("lon", "lat", "chan")
VMEM_BYTES = 67043328
EARLY_CUTS = 2


def one_hot(shape, test):
    rows = lax.broadcasted_iota(jnp.int32, shape, 0)
    cols = lax.broadcasted_iota(jnp.int32, shape, 1)
    return jnp.where(test(rows, cols), 1.0, 0.0).astype(BF16)


def share(rows, peers, unit):
    for size in range(unit, rows + 1, unit):
        if rows % size == 0 and rows // size <= peers:
            return size
    raise ValueError("no share")


class Plan:
    def __init__(self, sizes, fine_shape, cg_shape, kernel_shape):
        self.lon_n, self.lat_n, self.chan_n = (sizes[a] for a in AXES)
        self.h, self.w = fine_shape[0] // 2, fine_shape[1] // 2
        self.in_ch, self.out_ch = kernel_shape[2], kernel_shape[3]
        self.width = cg_shape[2]
        self.group = min(self.width, 32)
        self.units = self.width // self.group
        self.part = share(3 * self.group, self.lon_n, 8)
        self.owners = 3 * self.group // self.part
        self.cut = self.in_ch // self.lat_n
        self.fine_cuts = 4 if self.h % 4 == 0 else 1
        parcels = 3 + (self.chan_n - 1) * self.units
        self.remote = (
            2 + 2 + 2
            + (self.chan_n - 1) * (self.units + 1)
            + parcels * (self.lat_n + self.lon_n + 1)
            + self.units * (self.lon_n - 1)
            + self.units * self.lon_n * (self.chan_n - 1)
            + self.chan_n * self.units * (self.lat_n - 1)
        )


def grads_kernel(
    plan, scale,
    fine, cg, kernel, rows_out, kg_out,
    fbuf, kcat, tiles, xs, ev, tt, edge_out, edge_in, tedge_out, tedge_in,
    acc, land_lat, land_lon, land_x,
    fine_sem, kernel_sem, own_sem, halo_recv, send_sem, recv_sem,
):
    lon_n, lat_n, chan_n = plan.lon_n, plan.lat_n, plan.chan_n
    h, w, width, group, units = plan.h, plan.w, plan.width, plan.group, plan.units
    part, owners, out_ch, cut = plan.part, plan.owners, plan.out_ch, plan.cut
    sizes = {"lon": lon_n, "lat": lat_n, "chan": chan_n}
    me = {a: lax.axis_index(a) for a in AXES}
    lon, lat, chan = me["lon"], me["lat"], me["chan"]
    my_chunk = jnp.minimum(lon, owners - 1)
    is_owner = None if owners == lon_n else lon < owners

    def other(axis, step):
        return lax.rem(me[axis] + step + sizes[axis], sizes[axis])

    def channels(block, unit=0, size=None):
        start = pl.multiple_of(block * width + unit * group, PACK)
        return pl.ds(start, width if size is None else size)

    def guarded(condition, action):
        if condition is None:
            action()
        else:
            pl.when(condition)(action)

    step = h // plan.fine_cuts
    fine_in = []
    for k in range(plan.fine_cuts):
        at = pl.ds(k * step, step)
        fine_in.append(pltpu.make_async_copy(fine.at[at, 0], fbuf.at[at], fine_sem.at[k]))

    def first_row(p):
        return jnp.maximum(p * h - 1, 0), jnp.where(p > 0, 0, 1)

    own_from, own_to = first_row(chan)
    own_in = pltpu.make_async_copy(
        cg.at[pl.ds(own_from, h + 1)], tiles.at[pl.ds(own_to, h + 1), channels(chan)], own_sem.at[0]
    )
    inner = jnp.logical_and(chan > 0, chan < chan_n - 1)
    own_extra = pltpu.make_async_copy(
        cg.at[jnp.minimum((chan + 1) * h, chan_n * h - 1)], tiles.at[h + 1, channels(chan)], own_sem.at[1]
    )
    kernel_in = []
    for r in range(3):
        for s in range(3):
            n = 3 * r + s
            kernel_in.append(
                pltpu.make_async_copy(kernel.at[r, s], kcat.at[:, pl.ds(n * out_ch, out_ch)], kernel_sem.at[n])
            )
    barrier = pltpu.get_barrier_semaphore()
    greeted = 0
    for dl in range(lat_n):
        for dc in range(chan_n):
            if dl or dc:
                pl.semaphore_signal(
                    barrier, inc=1, device_id={"lat": other("lat", dl), "chan": other("chan", dc)}, device_id_type=MESH
                )
                greeted += 1
    for d in range(1, lon_n):
        pl.semaphore_signal(barrier, inc=1, device_id={"lon": other("lon", d)}, device_id_type=MESH)
        greeted += 1

    for copy in fine_in:
        copy.start()
    own_in.start()
    if chan_n > 2:
        pl.when(inner)(lambda: own_extra.start())
    for copy in kernel_in:
        copy.start()

    is_top = jnp.logical_and(lat == 0, chan == 0)
    is_bottom = jnp.logical_and(lat == lat_n - 1, chan == chan_n - 1)

    @pl.when(is_top)
    def _():
        tiles[0] = jnp.zeros(tiles.shape[1:], BF16)

    @pl.when(is_bottom)
    def _():
        tiles[h + 1] = jnp.zeros(tiles.shape[1:], BF16)

    def picked_column(row, col):
        s, j = row // LANES, row % LANES
        return jnp.logical_and(jnp.logical_and(col == 2 * (j + s - 1), j < w), col >= 0)

    pick = one_hot((3 * LANES, 2 * w), picked_column)

    def take_even(i, _):
        picked = jnp.dot(pick, fbuf[i], preferred_element_type=F32)
        at = pl.ds(pl.multiple_of(i * LANES, LANES), LANES)
        for s in range(3):
            ev[s, at, :] = picked[s * LANES:(s + 1) * LANES].astype(BF16)
        return 0

    def take_edges(rows):
        for i in rows:
            edge_out[1, pl.ds(i, 1), :] = fbuf[i, pl.ds(0, PACK), :].astype(F32)[0:1]
            edge_out[0, pl.ds(i, 1), :] = fbuf[i, pl.ds(2 * w - PACK, PACK), :].astype(F32)[PACK - 2:PACK - 1]

    def take_evens(cuts):
        for k in cuts:
            lax.fori_loop(k * step, (k + 1) * step, take_even, 0, unroll=2 - step % 2)

    for k in range(plan.fine_cuts):
        fine_in[k].wait()
        take_edges(range(k * step, (k + 1) * step))
    take_evens(range(EARLY_CUTS))

    pad = jnp.zeros((width, LANES - w), BF16) if w < LANES else None

    def fill(d, unit, size, which):
        at = pl.ds(d * width + unit * group, size)
        source = channels(other("chan", d), unit, size)
        for i in which:
            block = tiles[i, source, :]
            if pad is not None:
                block = jnp.concatenate([block, pad[:size]], axis=1)
            xs[at, pl.ds(i * LANES, LANES)] = block

    pl.semaphore_wait(barrier, greeted)

    sends = []

    def send(condition, src, dst, where, recv=None):
        n = len(sends)
        copy = pltpu.make_async_remote_copy(
            src_ref=src, dst_ref=dst, send_sem=send_sem.at[n], recv_sem=recv_sem.at[n] if recv is None else recv,
            device_id=where, device_id_type=MESH,
        )
        guarded(condition, lambda: copy.start())
        sends.append((condition, copy))
        return n

    def arrive(ref, n, condition=None):
        guarded(condition, lambda: pltpu.make_async_copy(ref, ref, recv_sem.at[n]).wait())

    def both(a, b):
        return b if a is None else a if b is None else jnp.logical_and(a, b)

    send(
        lat < lat_n - 1, cg.at[chan_n * h - 1], tiles.at[0, channels(chan)],
        {"lat": jnp.minimum(lat + 1, lat_n - 1), "chan": 0}, halo_recv.at[chan],
    )
    send(
        lat > 0, cg.at[0], tiles.at[h + 1, channels(chan)],
        {"lat": jnp.maximum(lat - 1, 0), "chan": chan_n - 1}, halo_recv.at[chan_n + chan],
    )
    edge_n = [
        send(None, edge_out.at[0], edge_in.at[0], {"lon": other("lon", 1)}),
        send(None, edge_out.at[1], edge_in.at[1], {"lon": other("lon", -1)}),
    ]
    tile_n = {}
    for d in range(1, chan_n):
        p = other("chan", -d)
        source, target = first_row(p)
        for u in range(units):
            tile_n[d, u] = send(
                None, cg.at[pl.ds(source, h + 1), pl.ds(u * group, group)],
                tiles.at[pl.ds(target, h + 1), channels(chan, u, group)], {"chan": p},
            )
        if chan_n > 2:
            tile_n[d] = send(
                jnp.logical_and(p > 0, p < chan_n - 1), cg.at[jnp.minimum((p + 1) * h, chan_n * h - 1)],
                tiles.at[h + 1, channels(chan)], {"chan": p},
            )

    def halo_arrive(d):
        block = other("chan", d)
        for row, n, condition in (
            (0, block, jnp.logical_and(chan == 0, lat > 0)),
            (h + 1, chan_n + block, jnp.logical_and(chan == chan_n - 1, lat < lat_n - 1)),
        ):
            ref = tiles.at[row, channels(block)]
            guarded(condition, lambda: pltpu.make_async_copy(ref, ref, halo_recv.at[n]).wait())

    def tiles_arrive(d, u):
        block = other("chan", d)
        _, target = first_row(chan)
        arrive(tiles.at[pl.ds(target, h + 1), channels(block, u, group)], tile_n[d, u])
        if u == 0:
            if chan_n > 2:
                arrive(tiles.at[h + 1, channels(block)], tile_n[d], inner)
            halo_arrive(d)

    def terms(d, first, count, s):
        pieces = []
        for u in range(first, first + count):
            for r in range(3):
                pieces.append(xs[pl.ds(d * width + u * group, group), pl.ds((2 - r) * LANES, h * LANES)])
        total = jnp.dot(jnp.concatenate(pieces, axis=0), ev[s], preferred_element_type=F32)
        for u in range(count):
            for k in range(owners):
                at = (u * owners + k) * part
                for half in range(lat_n):
                    acc[half, d * units + first + u, k, s] = total[at:at + part, half * cut:(half + 1) * cut]

    def lat_send(d, first, count, s0, s_n):
        g, s = pl.ds(d * units + first, count), pl.ds(s0, s_n)
        numbers = []
        for dl in range(1, lat_n):
            l = other("lat", dl)
            numbers.append(
                send(None, acc.at[l, g, :, s], land_lat.at[dl - 1, g, :, s], {"lat": l})
            )
        return numbers

    def lat_add(parcel, numbers):
        d, first, count, s0, s_n = parcel
        g, s = pl.ds(d * units + first, count), pl.ds(s0, s_n)
        for dl in range(1, lat_n):
            arrive(land_lat.at[dl - 1, g, :, s], numbers[dl - 1])
        total = acc[lat, g, :, s]
        for dl in range(1, lat_n):
            total = total + land_lat[dl - 1, g, :, s]
        acc[lat, g, :, s] = total
        result = []
        for dz in range(1, lon_n):
            k = other("lon", dz)
            result.append(
                send(
                    None if owners == lon_n else k < owners, acc.at[lat, g, jnp.minimum(k, owners - 1), s],
                    land_lon.at[dz - 1, g, s], {"lon": k},
                )
            )
        return result

    x_n = {}

    def lon_sum(parcel, numbers):
        d, first, count, s0, s_n = parcel
        g, s = pl.ds(d * units + first, count), pl.ds(s0, s_n)
        for dz in range(1, lon_n):
            arrive(land_lon.at[dz - 1, g, s], numbers[dz - 1], is_owner)
        total = acc[lat, g, my_chunk, s]
        for dz in range(1, lon_n):
            total = total + land_lon[dz - 1, g, s]
        return total

    def lon_add(parcel, numbers):
        d, first, count, s0, s_n = parcel
        g, s = pl.ds(d * units + first, count), pl.ds(s0, s_n)

        def add():
            acc[lat, g, my_chunk, s] = lon_sum(parcel, numbers)

        guarded(is_owner, add)
        x_n[parcel] = send(
            is_owner, acc.at[lat, g, my_chunk, s], land_x.at[d, pl.ds(first, count), s], {"chan": other("chan", d + 1)}
        )

    last = chan_n - 1
    mine = other("chan", last)
    z_n, fx_n, lat_n_of = {}, {}, {}

    def owner_of(dz):
        k = other("lon", -dz)
        return jnp.minimum(k, owners - 1), (None if owners == lon_n else k < owners)

    def forward(u, dz):
        k, there = owner_of(dz)
        at = kg_out.at[lat, mine, u, k]
        for e in range(1, chan_n):
            fx_n[u, dz, e] = send(there, at, at, {"chan": other("chan", e)})

    def finish(parcel, numbers):
        u = parcel[1]

        def add():
            total = lon_sum(parcel, numbers)
            for other_parcel, n in x_n.items():
                d, first, count, s0, s_n = other_parcel
                if first <= u < first + count and n not in done:
                    ref = land_x.at[d, pl.ds(first, count), pl.ds(s0, s_n)]
                    pltpu.make_async_copy(ref, ref, recv_sem.at[n]).wait()
                    done.append(n)
            total = total[0]
            for d in range(last):
                total = total + land_x[d, u]
            kg_out[lat, mine, u, my_chunk] = total * scale

        guarded(is_owner, add)
        at = kg_out.at[lat, mine, u, my_chunk]
        for dz in range(1, lon_n):
            z_n[u, dz] = send(is_owner, at, at, {"lon": other("lon", dz)})
        forward(u, 0)

    done = []

    def relay(u):
        for dz in range(1, lon_n):
            k, there = owner_of(dz)
            arrive(kg_out.at[lat, mine, u, k], z_n[u, dz], there)
            forward(u, dz)
        lat_forward(mine, u)

    def lat_forward(block, u):
        at = kg_out.at[lat, block, u]
        for dl in range(1, lat_n):
            n = send(None, at, at, {"lat": other("lat", dl)})
            lat_n_of[len(lat_n_of)] = (n, dl, block, u)

    def collect(u):
        for e in range(1, chan_n):
            block = other("chan", -e - 1)
            for dz in range(lon_n):
                k, there = owner_of(dz)
                arrive(kg_out.at[lat, block, u, k], fx_n[u, dz, e], there)
            lat_forward(block, u)

    def turned(row, col):
        s, j = row // w, row % w
        return col == j + 1 - s

    def make_taps():
        turn = one_hot((3 * w, w), turned)
        for i in range(0, h + 2, 2):
            pair = tiles[pl.ds(i, 2)].reshape(2 * out_ch, w)
            moved = lax.dot_general(turn, pair, (((1,), (1,)), ((), ())), preferred_element_type=F32)
            for k in range(2):
                lanes = slice(k * out_ch, (k + 1) * out_ch)
                for s in range(3):
                    tt[s, pl.ds((i + k) * w, w), :] = moved[s * w:(s + 1) * w, lanes].astype(BF16)
                tedge_out[0, pl.ds(i + k, 1), :] = moved[2 * w - 1:2 * w, lanes]
                tedge_out[1, pl.ds(i + k, 1), :] = moved[w:w + 1, lanes]

    def patch(buffer, base, row, value):
        start = base + row // PACK * PACK
        at = pl.ds(start, PACK)
        old = buffer[at, :].astype(F32)
        rows = lax.broadcasted_iota(jnp.int32, old.shape, 0)
        buffer[at, :] = jnp.where(rows == row % PACK, value, old).astype(BF16)

    def patch_even(i):
        base = i * LANES
        patch(ev.at[0], base, 0, edge_in[0, pl.ds(i, 1), :])
        patch(ev.at[2], base, w - 1, edge_in[1, pl.ds(i, 1), :])

    def patch_taps(i):
        base = i * w
        patch(tt.at[2], base, 0, tedge_in[0, pl.ds(i, 1), :])
        patch(tt.at[0], base, w - 1, tedge_in[1, pl.ds(i, 1), :])

    ig_rows, rim_rows = math.gcd(h, 4), math.gcd(h, 8)
    rim = (0, w - PACK)
    middle = ((PACK, w - 2 * PACK),)
    spread = one_hot((2 * w, w), lambda row, col: row == 2 * col)

    def products(first, count, spans):
        columns = []
        for r in range(3):
            for s in range(3):
                stack = []
                for k in range(count):
                    for start, size in spans:
                        at = pl.multiple_of((first + k + 2 - r) * w + start, PACK)
                        stack.append(tt[s, pl.ds(at, size), :])
                columns.append(jnp.concatenate(stack, axis=0))
        return lax.dot_general(
            jnp.concatenate(columns, axis=1), kcat[...], (((1,), (1,)), ((), ())), preferred_element_type=F32
        ).astype(BF16)

    def put(total, first, count, spans):
        size = sum(n for _, n in spans)
        for k in range(count):
            row = jnp.dot(
                spread[:2 * size, :size], total[k * size:(k + 1) * size], preferred_element_type=F32
            ).astype(BF16)
            taken = 0
            for start, n in spans:
                rows_out[first + k, pl.ds(2 * start, 2 * n), :] = row[2 * taken:2 * (taken + n)]
                taken += n

    def even_grads(b, _):
        put(products(b * ig_rows, ig_rows, middle), b * ig_rows, ig_rows, middle)
        return 0

    def rim_grads(b, _):
        spans = tuple((start, PACK) for start in rim)
        put(products(b * rim_rows, rim_rows, spans), b * rim_rows, rim_rows, spans)
        return 0

    blocks = h // ig_rows
    state = {"ig": 0}

    def some_even_grads(count):
        end = min(blocks, state["ig"] + count)
        if end > state["ig"]:
            lax.fori_loop(state["ig"], end, even_grads, 0)
        state["ig"] = end

    take_evens(range(EARLY_CUTS, plan.fine_cuts))
    own_in.wait()
    if chan_n > 2:
        pl.when(inner)(lambda: own_extra.wait())
    halo_arrive(0)
    fill(0, 0, width, range(h + 2))
    parcels = {}

    def begin(d, first, count, s0, s_n):
        parcel = (d, first, count, s0, s_n)
        for s in range(s0, s0 + s_n):
            terms(d, first, count, s)
        parcels[parcel] = lat_send(*parcel)
        return parcel

    a1 = begin(0, 0, units, 1, 1)
    parcels[a1] = lat_add(a1, parcels[a1])
    for n, ref in zip(edge_n, (edge_in.at[0], edge_in.at[1])):
        arrive(ref, n)
    for i in range(h):
        patch_even(i)
    a0 = begin(0, 0, units, 0, 1)
    a2 = begin(0, 0, units, 2, 1)
    parcels[a0] = lat_add(a0, parcels[a0])
    parcels[a2] = lat_add(a2, parcels[a2])
    own = [a1, a0, a2]
    early = []
    for d in range(1, chan_n):
        for u in range(units):
            tiles_arrive(d, u)
            fill(d, u, group, range(h + 2))
            parcel = begin(d, u, 1, 0, 3)
            early.append(parcel)
            parcels[parcel] = lat_add(parcel, parcels[parcel])
    finals = [q for q in early if q[0] == last]
    for parcel in own + early[:-len(finals)]:
        lon_add(parcel, parcels[parcel])
    make_taps()
    tedge_n = [
        send(None, tedge_out.at[0], tedge_in.at[0], {"lon": other("lon", 1)}),
        send(None, tedge_out.at[1], tedge_in.at[1], {"lon": other("lon", -1)}),
    ]
    for copy in kernel_in:
        copy.wait()
    some_even_grads(6)
    for parcel in finals[:-1]:
        finish(parcel, parcels[parcel])
    some_even_grads(0)
    finish(finals[-1], parcels[finals[-1]])
    some_even_grads(blocks)
    for n, ref in zip(tedge_n, (tedge_in.at[0], tedge_in.at[1])):
        arrive(ref, n)
    for i in range(h + 2):
        patch_taps(i)
    lax.fori_loop(0, h // rim_rows, rim_grads, 0)
    for parcel in finals[:-1]:
        relay(parcel[1])
    relay(finals[-1][1])
    for parcel in finals:
        collect(parcel[1])
    for n, dl, block, u in lat_n_of.values():
        there = other("lat", -dl)
        arrive(kg_out.at[there, block, u], n)
    for condition, copy in sends:
        guarded(condition, lambda: copy.wait_send())


def finish_kernel(plan, rows, kg_in, grad_out, kg_out, zeros, turned, sems, kg_sems):
    zero_rows = zeros.shape[0]
    groups = rows.shape[0] // zero_rows
    in_ch, part, group, cut = plan.in_ch, plan.part, plan.group, plan.cut
    writes = []
    for k in range(groups):
        at = pl.ds(k * zero_rows, zero_rows)
        writes.append(pltpu.make_async_copy(rows.at[at], grad_out.at[at, 0], sems.at[2 * k]))
        writes[-1].start()
    zeros[...] = jnp.zeros(zeros.shape, BF16)
    for k in range(groups):
        at = pl.ds(k * zero_rows, zero_rows)
        writes.append(pltpu.make_async_copy(zeros, grad_out.at[at, 1], sems.at[2 * k + 1]))
        writes[-1].start()
    for s in range(3):
        for half in range(plan.lat_n):
            pieces = [[], [], []]
            for p in range(plan.chan_n):
                for u in range(plan.units):
                    stack = jnp.concatenate([kg_in[half, p, u, k, s] for k in range(plan.owners)], axis=0)
                    for r in range(3):
                        pieces[r].append(stack[r * group:(r + 1) * group])
            for r in range(3):
                turned[3 * r + s, pl.ds(half * cut, cut), :] = jnp.concatenate(pieces[r], axis=0).T
        for r in range(3):
            n = 3 * r + s
            writes.append(
                pltpu.make_async_copy(turned.at[n], kg_out.at[pl.ds(n * in_ch, in_ch)], kg_sems.at[n])
            )
            writes[-1].start()
    for copy in writes:
        copy.wait()


def on_device(sizes, fine_act, coarse_grad, kernel):
    plan = Plan(sizes, fine_act.shape, coarse_grad.shape, kernel.shape)
    fine_rows, fine_cols, in_ch = fine_act.shape
    h, w, out_ch = plan.h, plan.w, plan.out_ch
    scale = 1.0 / math.sqrt(h * plan.lat_n * plan.chan_n * w * plan.lon_n)
    cg = jnp.transpose(coarse_grad, (0, 2, 1))
    fine = fine_act.reshape(h, 2, fine_cols, in_ch)
    dma = pltpu.SemaphoreType.DMA
    vmem = pl.BlockSpec(memory_space=pltpu.VMEM)
    hbm = pl.BlockSpec(memory_space=pltpu.HBM)
    sums = plan.chan_n * plan.units
    chunk = (3, plan.part, plan.cut)
    rows_shape = (h, fine_cols, in_ch)
    kg_shape = (plan.lat_n, plan.chan_n, plan.units, plan.owners) + chunk
    edge_rows = -(-(h + 2) // 8) * 8
    held = 2 * math.prod(rows_shape) + 4 * math.prod(kg_shape)
    rows, kg = pl.pallas_call(
        functools.partial(grads_kernel, plan, scale),
        out_shape=(pltpu.VMEM(rows_shape, BF16), pltpu.VMEM(kg_shape, F32)),
        in_specs=[hbm, hbm, hbm],
        out_specs=(vmem, vmem),
        scratch_shapes=[
            pltpu.VMEM((h, fine_cols, in_ch), BF16),
            pltpu.VMEM((in_ch, 9 * out_ch), BF16),
            pltpu.VMEM((h + 2, out_ch, w), BF16),
            pltpu.VMEM((out_ch, (h + 2) * LANES), BF16),
            pltpu.VMEM((3, h * LANES, in_ch), BF16),
            pltpu.VMEM((3, (h + 2) * w, out_ch), BF16),
            pltpu.VMEM((2, edge_rows, in_ch), F32),
            pltpu.VMEM((2, edge_rows, in_ch), F32),
            pltpu.VMEM((2, edge_rows, out_ch), F32),
            pltpu.VMEM((2, edge_rows, out_ch), F32),
            pltpu.VMEM((plan.lat_n, sums, plan.owners) + chunk, F32),
            pltpu.VMEM((plan.lat_n - 1, sums, plan.owners) + chunk, F32),
            pltpu.VMEM((plan.lon_n - 1, sums) + chunk, F32),
            pltpu.VMEM((plan.chan_n - 1, plan.units) + chunk, F32),
            dma((plan.fine_cuts,)),
            dma((9,)),
            dma((2,)),
            dma((2 * plan.chan_n,)),
            dma((plan.remote,)),
            dma((plan.remote,)),
        ],
        compiler_params=pltpu.CompilerParams(
            collective_id=0, has_side_effects=True, vmem_limit_bytes=(VMEM_BYTES - held) // 65536 * 65536
        ),
        name="grads",
    )(fine, cg, kernel)
    zero_rows = math.gcd(h, 8)
    input_grad, kernel_grad = pl.pallas_call(
        functools.partial(finish_kernel, plan),
        out_shape=(
            jax.ShapeDtypeStruct((h, 2, fine_cols, in_ch), BF16),
            jax.ShapeDtypeStruct((9 * in_ch, out_ch), F32),
        ),
        in_specs=[vmem, vmem],
        out_specs=(hbm, hbm),
        scratch_shapes=[
            pltpu.VMEM((zero_rows, fine_cols, in_ch), BF16),
            pltpu.VMEM((9, in_ch, out_ch), F32),
            dma((2 * (h // zero_rows),)),
            dma((9,)),
        ],
        compiler_params=pltpu.CompilerParams(vmem_limit_bytes=VMEM_BYTES // 4),
        name="finish",
    )(rows, kg)
    return (input_grad.reshape(fine_act.shape), kernel_grad.reshape(3, 3, in_ch, out_ch))


def solution(mesh):
    placed = (P(("parts", "lat", "chan"), "lon", None), P(("parts", "lat"), "lon", "chan"), P())
    sizes = {axis: mesh.shape[axis] for axis in AXES}
    return jax.shard_map(
        functools.partial(on_device, sizes),
        mesh=mesh,
        in_specs=placed,
        out_specs=(P(("parts", "lat", "chan"), "lon", None), P("parts", None, None, None)),
        check_vma=False,
    )
```
